32 devices in a mesh: visit: 8 (over z, core), grp: 4 (over y, x).
Axes of the slice: x: 2, y: 2, z: 4, core: 2. Of those that a mesh axis runs over, the one named last changes fastest.
Arguments:
- coadd_tiles: float32 [2048, 8192], P('visit', 'grp'), may hold values from -9 to 9
- science: float32 [2048, 8192], P('visit', 'grp'), may hold values from -16 to 16
- correlation: int32 [8], P('visit'), may hold values from 0 to 7, as said below
- offset: int32 [8], P('visit'), may hold values from 10 to 246
Outputs:
- difference: float32 [2048, 8192], P('visit', 'grp')
- significance: float32 [2048, 8192], P('visit', 'grp')
- match_coef: float32 [8, 6], P('visit')
The draws below stay inside these ranges and needn't reach their ends.
Inputs may be any that keep to these rules, and one draw needn't show every extreme that they name: correlation is a permutation of 0 .. 7.
All inputs are finite; a program needn't handle non-finite values.
Results may differ from the reference program's by a relative error of at most 0.0003.
Values sent between devices are 32-bit elements; how exact they have to be, the bound alone decides.
A program may use at most 128 MiB of HBM per device.

```python
import jax
import jax.numpy as jnp
from jax import lax

ROWS = 256
COLS = 2048
KER_HALF = 10
BASIS = 5
FILT_HALF = 6
N_VISIT = 8
N_GRP = 4


def sky_tiles(key):
    layout = (N_VISIT * ROWS, N_GRP * COLS)
    values = jax.random.truncated_normal(jax.random.fold_in(key, 11), -5.0, 5.0, layout, jnp.float32)
    stripe = (jnp.arange(N_GRP * COLS) // COLS).astype(jnp.float32)
    amplitude = 3.0 ** (0.5 * stripe / max(N_GRP - 1, 1))
    return values * amplitude[None, :]


def sky_table(key):
    ordering = jax.random.permutation(jax.random.fold_in(key, 12), N_VISIT).astype(jnp.int32)
    shifts = jax.random.randint(jax.random.fold_in(key, 13), (N_VISIT,), KER_HALF, ROWS - KER_HALF + 1).astype(jnp.int32)
    chosen = jax.random.permutation(jax.random.fold_in(key, 18), N_VISIT).astype(jnp.int32)
    shifts = shifts.at[chosen[0]].set(ROWS - KER_HALF)
    shifts = shifts.at[chosen[1]].set(KER_HALF)
    return (ordering, shifts.astype(jnp.int32))


def draw_coadd_tiles(key, part):
    return sky_tiles(key)


def draw_correlation(key, part):
    return sky_table(key)[0]


def draw_offset(key, part):
    return sky_table(key)[1]


def draw_science(key, part):
    coadd_tiles = sky_tiles(key)
    ordering, shifts = sky_table(key)
    padded = jnp.pad(coadd_tiles, ((0, 0), (KER_HALF, KER_HALF)))
    spreads = jax.random.uniform(jax.random.fold_in(key, 14), (N_VISIT,), jnp.float32, 1.2, 2.6)
    gains = jnp.exp(jax.random.uniform(jax.random.fold_in(key, 15), (N_VISIT, N_GRP), jnp.float32, jnp.log(0.6), jnp.log(1.6)))
    levels = jax.random.uniform(jax.random.fold_in(key, 16), (N_VISIT, N_GRP), jnp.float32, -0.5, 0.5)
    noise = 0.1 * jax.random.truncated_normal(jax.random.fold_in(key, 17), -5.0, 5.0, (N_VISIT, ROWS, N_GRP * COLS), jnp.float32)
    points = jnp.arange(-KER_HALF, KER_HALF + 1).astype(jnp.float32)

    def exposure(inputs):
        tile_id, shift_rows, spread = inputs
        rows_index = (tile_id * ROWS + shift_rows - KER_HALF + jnp.arange(ROWS + 2 * KER_HALF).astype(jnp.int32)) % (N_VISIT * ROWS)
        window = jnp.take(padded, rows_index.astype(jnp.int32), axis=0)
        kernel_taps = jnp.exp(-points * points / (2.0 * spread * spread))
        kernel_taps = kernel_taps / jnp.sum(kernel_taps)
        blurred = lax.conv_general_dilated(window[None, None], kernel_taps[None, None, None, :], (1, 1), 'VALID')
        blurred = lax.conv_general_dilated(blurred, kernel_taps[None, None, :, None], (1, 1), 'VALID')
        return blurred[0, 0]
    blurred = lax.map(exposure, (ordering, shifts, spreads))
    stripe = jnp.arange(N_GRP * COLS) // COLS
    gain_cols = jnp.take(gains, stripe, axis=1)
    level_cols = jnp.take(levels, stripe, axis=1)
    result = blurred * gain_cols[:, None, :] + level_cols[:, None, :] + noise
    return result.reshape(N_VISIT * ROWS, N_GRP * COLS)


def setup_inputs(seed: int = 0) -> dict:
    keys = jax.random.split(jax.random.key(seed), 5)
    coadd_tiles = draw_coadd_tiles(jax.random.fold_in(keys[4], 71), 0)
    science = draw_science(jax.random.fold_in(keys[4], 71), 0)
    correlation = draw_correlation(jax.random.fold_in(keys[4], 71), 0)
    offset = draw_offset(jax.random.fold_in(keys[4], 71), 0)
    return dict(coadd_tiles=coadd_tiles, science=science, correlation=correlation, offset=offset)


ridge = 0.05
epsilon = 1e-06

def gauss_taps(spread, half_width):
    points = jnp.arange(-half_width, half_width + 1).astype(jnp.float32)
    return jnp.exp(-points * points / (2.0 * spread * spread))

def basis_taps():
    points = jnp.arange(-KER_HALF, KER_HALF + 1).astype(jnp.float32)
    narrow = gauss_taps(1.0, KER_HALF)
    middle = gauss_taps(1.8, KER_HALF)
    wide_gauss = gauss_taps(3.2, KER_HALF)
    slope_taps = points * middle / 1.8
    row_taps = jnp.stack([narrow, middle, wide_gauss, slope_taps, middle])
    col_taps = jnp.stack([narrow, middle, wide_gauss, middle, slope_taps])
    scales = jnp.sqrt(lax.optimization_barrier(jnp.sum(row_taps * row_taps, 1)) * lax.optimization_barrier(jnp.sum(col_taps * col_taps, 1)))
    return (row_taps / scales[:, None], col_taps)

def filter_taps():
    smooth = gauss_taps(2.0, FILT_HALF)
    return smooth / jnp.sqrt(jnp.sum(smooth * smooth))

def along_cols_ref(image_in, kernel_taps):
    result = lax.conv_general_dilated(image_in[None, None], kernel_taps[:, None, None, :], (1, 1), 'VALID', precision=lax.Precision.HIGHEST)
    return result[0]

def along_rows_ref(layers, kernel_taps):
    result = lax.conv_general_dilated(layers[None], kernel_taps[:, None, :, None], (1, 1), 'VALID', feature_group_count=layers.shape[0], precision=lax.Precision.HIGHEST)
    return result[0]

def build_normal(gram_matrix, basis_sums, counted):
    upper_rows = jnp.concatenate([gram_matrix, basis_sums[:, None]], 1)
    lower_row = jnp.concatenate([basis_sums, jnp.array([counted], jnp.float32)])[None]
    return jnp.concatenate([upper_rows, lower_row], 0) / counted + ridge * jnp.eye(BASIS + 1, dtype=jnp.float32)

def reference(coadd_tiles, science, correlation, offset):
    row_taps, col_taps = basis_taps()
    smooth = filter_taps()[None]
    strip_rows = N_VISIT * ROWS
    padded = jnp.pad(coadd_tiles, ((0, 0), (KER_HALF, KER_HALF)))
    counted = float(ROWS * COLS * N_GRP)

    def exposure(inputs):
        tile_id, shift_rows, science_rows = inputs
        first_row = tile_id * ROWS + shift_rows - KER_HALF
        rows_index = (first_row + jnp.arange(ROWS + 2 * KER_HALF).astype(jnp.int32)) % strip_rows
        window = jnp.take(padded, rows_index.astype(jnp.int32), axis=0)
        matched = along_rows_ref(along_cols_ref(window, col_taps), row_taps)
        basis_flat = matched.reshape(BASIS, -1)
        gram_matrix = jnp.dot(basis_flat, basis_flat.T, precision=lax.Precision.HIGHEST)
        basis_sums = lax.optimization_barrier(jnp.sum(basis_flat, 1))
        projection = jnp.dot(basis_flat, science_rows.reshape(-1), precision=lax.Precision.HIGHEST)
        science_total = jnp.sum(science_rows)
        normal = build_normal(gram_matrix, basis_sums, counted)
        rhs_vector = jnp.concatenate([projection, science_total[None]]) / counted
        coefficients = jnp.linalg.solve(normal, rhs_vector)
        difference = science_rows - lax.optimization_barrier(jnp.sum(coefficients[:BASIS, None, None] * matched, 0)) - coefficients[BASIS]
        wide_diff = jnp.pad(difference, ((FILT_HALF, FILT_HALF), (FILT_HALF, FILT_HALF)))
        filtered = along_rows_ref(along_cols_ref(wide_diff, smooth), smooth)[0]
        noise_power = lax.optimization_barrier(jnp.mean((difference * difference).reshape(ROWS, N_GRP, COLS), axis=(0, 2)))
        significance = filtered.reshape(ROWS, N_GRP, COLS) / jnp.sqrt(noise_power + epsilon)[None, :, None]
        return (difference, significance.reshape(ROWS, N_GRP * COLS), coefficients)
    differences, significances, coefficients = lax.map(exposure, (correlation, offset, science.reshape(N_VISIT, ROWS, N_GRP * COLS)))
    return (differences.reshape(strip_rows, N_GRP * COLS), significances.reshape(strip_rows, N_GRP * COLS), coefficients)
```

```python
import jax
import jax.numpy as jnp
from jax import lax
from jax.sharding import PartitionSpec as P

ROWS = 256
COLS = 2048
KER_HALF = 10
BASIS = 5
FILT_HALF = 6


ridge = 0.05
epsilon = 1e-06


def extended(x, sides, width):
    for axis, dim in sides:
        size, length = (lax.axis_size(axis), x.shape[dim])
        up = [(i, (i + 1) % size) for i in range(size - 1)]
        down = [(j, i) for i, j in up]
        last = lax.slice_in_dim(x, length - width, length, axis=dim)
        initial = lax.slice_in_dim(x, 0, width, axis=dim)
        before = lax.ppermute(last, axis, up)
        after = lax.ppermute(initial, axis, down)
        x = jnp.concatenate([before, x, after], axis=dim)
    return x


def gauss_taps(spread, half_width):
    points = jnp.arange(-half_width, half_width + 1).astype(jnp.float32)
    return jnp.exp(-points * points / (2.0 * spread * spread))


def basis_taps():
    points = jnp.arange(-KER_HALF, KER_HALF + 1).astype(jnp.float32)
    narrow = gauss_taps(1.0, KER_HALF)
    middle = gauss_taps(1.8, KER_HALF)
    wide_gauss = gauss_taps(3.2, KER_HALF)
    slope_taps = points * middle / 1.8
    row_taps = jnp.stack([narrow, middle, wide_gauss, slope_taps, middle])
    col_taps = jnp.stack([narrow, middle, wide_gauss, middle, slope_taps])
    scales = jnp.sqrt(jnp.sum(row_taps * row_taps, 1) * jnp.sum(col_taps * col_taps, 1))
    return (row_taps / scales[:, None], col_taps)


def filter_taps():
    smooth = gauss_taps(2.0, FILT_HALF)
    return smooth / jnp.sqrt(jnp.sum(smooth * smooth))


def taps_matrix(kernel_taps, step_len):
    half_width = (kernel_taps.shape[1] - 1) // 2
    input_pos = jnp.arange(step_len + 2 * half_width)[:, None]
    output_pos = jnp.arange(step_len)[None, :]
    distance = input_pos - output_pos
    result = jnp.zeros((kernel_taps.shape[0],) + distance.shape, jnp.float32)
    for tap in range(2 * half_width + 1):
        result = jnp.where((distance == tap)[None], kernel_taps[:, tap][:, None, None], result)
    return result


def block_anchors(extent, step_len):
    anchors = list(range(0, extent - step_len + 1, step_len))
    leftover = extent - (anchors[-1] + step_len)
    return (anchors, leftover)


def joined(result, axis_pos):
    layout = result.shape
    merged = layout[:axis_pos] + (-1,) + layout[axis_pos + 2 :]
    return result.reshape(merged)


def along_cols(image_in, kernel_taps):
    half_width = (kernel_taps.shape[1] - 1) // 2
    extent = image_in.shape[1] - 2 * half_width
    step_len = min(256, extent)
    anchors, leftover = block_anchors(extent, step_len)
    windows = jnp.stack(
        [image_in[:, anchor : anchor + step_len + 2 * half_width] for anchor in anchors], 1
    )
    result = jnp.einsum(
        "hnk,ckm->chnm",
        windows,
        taps_matrix(kernel_taps, step_len),
        precision=lax.Precision.HIGHEST,
    )
    return joined(result, 2)


def along_rows(layers, kernel_taps):
    half_width = (kernel_taps.shape[1] - 1) // 2
    extent = layers.shape[1] - 2 * half_width
    step_len = min(256, extent)
    anchors, leftover = block_anchors(extent, step_len)
    windows = jnp.stack([layers for anchor in anchors], 1)
    result = jnp.einsum(
        "cnkw,ckm->cnmw",
        windows,
        taps_matrix(kernel_taps, step_len),
        precision=lax.Precision.HIGHEST,
    )
    return joined(result, 1)


def build_normal(gram_matrix, basis_sums, counted):
    upper_rows = jnp.concatenate([gram_matrix, basis_sums[:, None]], 1)
    lower_row = jnp.concatenate([basis_sums, jnp.array([counted], jnp.float32)])[None]
    return jnp.concatenate([upper_rows, lower_row], 0) / counted + ridge * jnp.eye(
        BASIS + 1, dtype=jnp.float32
    )


def shards(coadd_tiles, science, correlation, offset):
    row_taps, col_taps = basis_taps()
    smooth = filter_taps()[None]
    visits = lax.axis_size("visit")
    groups = lax.axis_size("grp")
    span_rows = ROWS + 2 * KER_HALF
    tile_rows, tile_cols = coadd_tiles.shape
    strip = lax.all_to_all(coadd_tiles, "visit", split_axis=1, concat_axis=0, tiled=True)
    places = lax.all_gather(
        correlation * tile_rows + offset - KER_HALF, "visit", axis=0, tiled=True
    )
    strip = jnp.concatenate([strip, strip[:span_rows]], 0)
    outgoing = jnp.stack(
        [
            lax.dynamic_slice_in_dim(strip, places[v] % (visits * tile_rows), span_rows, 0)
            for v in range(visits)
        ],
        0,
    )
    window = lax.all_to_all(outgoing, "visit", split_axis=0, concat_axis=2, tiled=True)[0]
    margin = KER_HALF
    framed = extended(window, (("grp", 1),), margin)
    matched = along_rows(along_cols(framed, col_taps), row_taps)
    basis_flat = matched.reshape(BASIS, -1)
    gram_matrix = jnp.dot(basis_flat, basis_flat.T, precision=lax.Precision.HIGHEST)
    basis_sums = jnp.sum(basis_flat, 1)
    projection = jnp.dot(basis_flat, science.reshape(-1), precision=lax.Precision.HIGHEST)
    science_total = jnp.sum(science)
    gram_matrix, basis_sums, projection, science_total = lax.psum(
        (gram_matrix, basis_sums, projection, science_total), "grp"
    )
    counted = float(ROWS * COLS * groups)
    normal = build_normal(gram_matrix, basis_sums, counted)
    rhs_vector = jnp.concatenate([projection, science_total[None]]) / counted
    factor = jnp.linalg.cholesky(normal)
    halfway = lax.linalg.triangular_solve(factor, rhs_vector[:, None], left_side=True, lower=True)
    coefficients = lax.linalg.triangular_solve(
        factor, halfway, left_side=True, lower=True, transpose_a=True
    )[:, 0]
    difference = (
        science - jnp.sum(coefficients[:BASIS, None, None] * matched, 0) - coefficients[BASIS]
    )
    spread_diff = extended(difference, (("grp", 1),), FILT_HALF)
    row_framed = jnp.pad(spread_diff, ((FILT_HALF, FILT_HALF), (0, 0)))
    filtered = along_rows(along_cols(row_framed, smooth), smooth)[0]
    noise_power = jnp.mean(difference * difference)
    significance = filtered / jnp.sqrt(noise_power + epsilon)
    return (difference, significance, coefficients[None])


def solution(mesh):
    in_specs = (P("visit", "grp"), P("visit", "grp"), P("visit"), P("visit"))
    out_specs = (P("visit", "grp"), P("visit", "grp"), P("visit", None))
    return jax.shard_map(shards, mesh=mesh, in_specs=in_specs, out_specs=out_specs, check_vma=False)
```
